256 devices in a mesh: curves: 64 (over y, z_hi, x, core), primes: 4 (over z_lo).
Axes of the slice: x: 4, y: 4, z: 8 (z_hi: 2, z_lo: 4; z = z_hi * 4 + z_lo), core: 2. Of those that a mesh axis runs over, the one named last changes fastest.
Arguments:
- traces: int32 [32768, 24576], P('curves', 'primes'), may hold values from -724 to 724, as said below
- primes: int32 [24576], P('primes'), may hold values from 2 to 131071, as said below
- family: int32 [32768], P('curves'), may hold values from 0 to 1023
- log_conductor: float32 [32768], P('curves'), may hold values from 8 to 24
Outputs:
- profile: float32 [1024, 256], P('curves')
The draws below stay inside these ranges and needn't reach their ends.
Inputs may be any that keep to these rules, and one draw needn't show every extreme that they name: `primes`: every value is a prime below 131072. traces[c, k] squared is at most 4 primes[k].
All inputs are finite; a program needn't handle non-finite values.
Results may differ from the reference program's by a relative error of at most 0.0038.
Values sent between devices are 32-bit elements; how exact they have to be, the bound alone decides.
A program may use at most 64 MiB of HBM per device.

```python
import math
import jax
import jax.numpy as jnp
import numpy as np
from jax import lax

HEIGHTS = 128
CUR_DEV = 512
CURVES = 32768
PRIMES = 24576
FAM = 1024


def prime_tables():
    composite = np.zeros(131072, dtype=np.bool_)
    composite[:2] = True
    for number in range(2, 363):
        if not composite[number]:
            composite[number * number::number] = True
    prime_list = np.arange(131072, dtype=np.int64)[~composite]
    hasse_bound = np.floor(np.sqrt(4.0 * prime_list)).astype(np.int64)
    hasse_bound = hasse_bound - (hasse_bound * hasse_bound > 4 * prime_list)
    hasse_bound = hasse_bound + ((hasse_bound + 1) * (hasse_bound + 1) <= 4 * prime_list)
    return (prime_list.astype(np.int32), hasse_bound.astype(np.int32))


def prime_draw(key):
    prime_list, hasse_bound = prime_tables()
    count = prime_list.shape[0]
    picks = jax.random.randint(jax.random.fold_in(key, 7), (PRIMES,), 0, count)
    picks = picks.at[0].set(count - 1).at[1].set(0)
    return (jnp.asarray(prime_list)[picks], jnp.asarray(hasse_bound)[picks])


def draw_primes(key, part):
    return prime_draw(key)[0]


def draw_traces(key, part):
    chosen, limits = prime_draw(key)
    values = jax.random.randint(jax.random.fold_in(key, 11), (CURVES, PRIMES), -limits[None, :], limits[None, :] + 1)
    return values.at[0, 0].set(limits[0]).at[1, 0].set(-limits[0])


def with_ends(drawn, stream_key, low, high):
    shape = drawn.shape
    index_at = [jax.random.randint(jax.random.fold_in(stream_key, axis), (), 0, shape[axis]) for axis in range(len(shape))]
    drawn = drawn.at[tuple(index_at)].set(low)
    longest = shape.index(max(shape))
    index_at[longest] = (index_at[longest] + 1) % shape[longest]
    return drawn.at[tuple(index_at)].set(high)


def block_levels(stream_key, extent, pieces, least, largest):
    def one(axis_at, shards_of):
        steps = jax.random.uniform(jax.random.fold_in(jax.random.fold_in(stream_key, 6), axis_at), (shards_of,), jnp.float32, least / len(pieces), largest / len(pieces))
        return jnp.repeat(jnp.exp(steps), extent[axis_at] // shards_of).reshape((-1,) + (1,) * (len(extent) - axis_at - 1))

    level = one(*pieces[0])
    for cut in pieces[1:]:
        level = level * one(*cut)
    return level


def cumulative_ranks(amount, slope):
    portions = [(1 << 20) // math.isqrt(grade ** slope) + 1 for grade in range(1, amount + 1)]
    scale = 1 + sum(portions) // (1 << 30)
    return np.cumsum(np.array([max(1, weight // scale) for weight in portions]))


def ranked_ids(own_key, shape, amount, slope):
    table = cumulative_ranks(amount, slope)
    pick = jax.random.randint(jax.random.fold_in(own_key, 1), shape, 0, int(table[amount - 1]))
    grade = jnp.searchsorted(jnp.asarray(table, jnp.int32), pick, side="right")
    return jax.random.permutation(jax.random.fold_in(own_key, 2), amount)[grade].astype(jnp.int32)


def setup_inputs(seed: int = 0) -> dict:
    keys = jax.random.split(jax.random.key(seed), 5)
    traces = draw_traces(jax.random.fold_in(keys[4], 71), 0)
    primes = draw_primes(jax.random.fold_in(keys[4], 71), 0)
    family = with_ends(ranked_ids(keys[2], (CURVES,), FAM, 2), jax.random.fold_in(keys[2], 3), 0, FAM - 1).astype(jnp.int32)
    log_conductor = jnp.clip(jnp.exp(math.log(24.0) - 1.0986123 * jax.random.uniform(keys[3], (CURVES,), jnp.float32) ** block_levels(keys[3], (CURVES,), ((0, 64),), -0.2, 0.2)), 8.0, 24.0)
    return dict(traces=traces, primes=primes, family=family, log_conductor=log_conductor)


def reference(traces, primes, family, log_conductor):
    log_prime = jnp.log(primes.astype(jnp.float32))
    heights = (jnp.arange(HEIGHTS).astype(jnp.float32) + 1.0) * 0.5
    angles = log_prime[:, None] * heights[None, :]
    tables = jnp.concatenate([jnp.cos(angles), jnp.sin(angles)], axis=1).astype(jnp.bfloat16)
    weight = log_prime / primes.astype(jnp.float32)
    blocks = CURVES // CUR_DEV
    trace_blocks = traces.reshape(blocks, CUR_DEV, PRIMES)
    family_blocks = family.reshape(blocks, CUR_DEV)
    conductor_blocks = log_conductor.reshape(blocks, CUR_DEV)
    labels = jnp.arange(FAM).astype(jnp.int32)

    def step(carry, items):
        block_traces, block_family, block_conductor = items
        coefficient = (block_traces.astype(jnp.float32) * weight[None, :]).astype(jnp.bfloat16)
        totals = jnp.dot(coefficient, tables, preferred_element_type=jnp.float32)
        density = totals * (-2.0 / block_conductor)[:, None]
        onehot = (block_family[:, None] == labels[None, :]).astype(jnp.float32)
        sums = carry[0] + jnp.dot(onehot.T, density, precision=lax.Precision.HIGHEST, preferred_element_type=jnp.float32)
        counts = carry[1] + lax.optimization_barrier(jnp.sum(onehot, axis=0))
        return ((sums, counts), None)
    start = (jnp.zeros((FAM, 2 * HEIGHTS), jnp.float32), jnp.zeros((FAM,), jnp.float32))
    (sums, counts), _ = lax.scan(step, start, (trace_blocks, family_blocks, conductor_blocks))
    return sums / jnp.sqrt(jnp.maximum(counts, 1.0))[:, None]
```

```python
import jax
import jax.numpy as jnp
from jax import lax
from jax.experimental import pallas as pl
from jax.experimental.pallas import tpu as pltpu
from jax.sharding import PartitionSpec as P

MESH = pl.DeviceIdType.MESH
HEIGHTS = 128
ROWS = 512
DEPTH = 6144
CHUNK = 1024
STEPS = DEPTH // CHUNK
GROUPS = CHUNK // 128
FAMILIES = 1024
F32 = jnp.float32
BF16 = jnp.bfloat16


def times(a, b):
    return a[0] * b[0] - a[1] * b[1], a[0] * b[1] + a[1] * b[0]


def one_hot(cond):
    return jnp.where(cond, 1.0, 0.0).astype(BF16)


def kernel(
    traces, primes, family, conductor, out,
    tr, base_cos, base_sin, weight, table, total, factor, hot, rhs, send0, recv0, family2,
    sendx0, sendx1, recvx0, recvx1, sendy0, sendy1, recvy0, recvy1, sendz, recvz,
    copy_sem, ssem0, rsem0, ssem1, rsem1, ssem2, rsem2, ssem3, rsem3,
):
    me = lax.axis_index("curves")
    zl = lax.axis_index("primes")
    core = lax.rem(me, 2)
    x = lax.rem(lax.div(me, 2), 4)
    zh = lax.rem(lax.div(me, 8), 2)
    y = lax.div(me, 16)

    def curve(y, zh, x, core):
        return ((y * 2 + zh) * 4 + x) * 2 + core

    def along_x(p):
        return (curve(y, zh, lax.rem(x + p, 4), core), zl)

    def along_y(p):
        return (curve(lax.rem(y + p, 4), zh, x, core), zl)

    spot = (zh * 4 + zl) * 2 + core

    def along_z(p):
        q = lax.rem(spot + p, 16)
        return (curve(y, lax.div(q, 8), x, lax.rem(q, 2)), lax.rem(lax.div(q, 2), 4)), q

    sibling = (curve(y, zh, x, 1 - core), zl)

    def fetch(i):
        return pltpu.make_async_copy(traces.at[:, pl.ds(i * CHUNK, CHUNK)], tr.at[i], copy_sem.at[i])

    for i in range(STEPS):
        fetch(i).start()

    barrier = pltpu.get_barrier_semaphore()
    peers = [along_x(p) for p in (1, 2, 3)] + [along_y(p) for p in (1, 2, 3)] + [along_z(p)[0] for p in range(1, 16)]
    for peer in peers:
        pl.semaphore_signal(barrier, inc=1, device_id=peer, device_id_type=MESH)

    prime = primes[...].astype(F32)
    log_prime = jnp.log(prime)
    weight[...] = log_prime / prime
    base_cos[...] = jnp.cos(log_prime * 0.5)
    base_sin[...] = jnp.sin(log_prime * 0.5)
    total[...] = jnp.zeros_like(total)

    def labels(half):
        at = lax.broadcasted_iota(jnp.int32, (512, 128), 0)
        r, k, h = at & 7, (at >> 3) & 1, (at >> 4) & 1
        second, first = (at >> 5) & 3, (at >> 7) & 3
        xs, ys = (first, second) if half == 0 else (second, first)
        return (((ys * 2 + h) * 4 + xs) * 2 + k) * 16 + half * 8 + r

    label = [labels(0), labels(1)]

    def fill_hot(ref, base):
        for g in range(4):
            row = jnp.broadcast_to(ref[g:g + 1, :], (512, 128))
            for half in (0, 1):
                hot[half * 512:half * 512 + 512, (base + g) * 128:(base + g) * 128 + 128] = one_hot(label[half] == row)

    fill_hot(family, 0)
    inverse = -2.0 / conductor[...]
    for g in range(4):
        factor[g * 128:g * 128 + 128, :] = jnp.transpose(jnp.broadcast_to(inverse[g:g + 1, :], (128, 128)))

    sub = lax.broadcasted_iota(jnp.int32, (8, 128), 0)
    bits = [(sub & 1) != 0, (sub & 2) != 0, (sub & 4) != 0]

    def pick(mask, a):
        return jnp.where(mask, a[0], 1.0), jnp.where(mask, a[1], 0.0)

    def tables(row, lane):
        z = (jnp.broadcast_to(base_cos[pl.ds(row, 1), :], (8, 128)), jnp.broadcast_to(base_sin[pl.ds(row, 1), :], (8, 128)))
        z2 = times(z, z)
        z4 = times(z2, z2)
        powers = [times(times(z, pick(bits[0], z)), times(pick(bits[1], z2), pick(bits[2], z4)))]
        step = times(z4, z4)
        for _ in range(4):
            powers = powers + [times(a, step) for a in powers]
            step = times(step, step)
        for q in range(0, 16, 2):
            for part in (0, 1):
                both = jnp.concatenate([powers[q][part], powers[q + 1][part]], axis=0)
                table[part * 128 + q * 8:part * 128 + q * 8 + 16, lane:lane + 128] = both.astype(BF16)

    def trace_step(i, carry):
        for g in range(GROUPS):
            tables(i * GROUPS + g, g * 128)
        fetch(i).wait()
        w = jnp.concatenate([weight[pl.ds(i * GROUPS + g, 1), :] for g in range(GROUPS)], axis=1)
        coefficient = (tr[i].astype(F32) * w).astype(BF16)
        total[...] += lax.dot_general(coefficient, table[...], (((1,), (1,)), ((), ())), preferred_element_type=F32)
        return carry

    lax.fori_loop(0, STEPS - 1, trace_step, 0)

    pl.semaphore_wait(barrier, len(peers))
    families = pltpu.make_async_remote_copy(
        family, family2, ssem0.at[0], rsem0.at[0], device_id=sibling, device_id_type=MESH
    )
    families.start()
    trace_step(STEPS - 1, 0)

    def density(k):
        return total[:, pl.ds(pl.multiple_of(k * 128, 128), 128)] * factor[...]

    send0[...] = density(1 - core)
    columns = pltpu.make_async_remote_copy(
        send0, recv0, ssem0.at[1], rsem0.at[1], device_id=sibling, device_id_type=MESH
    )
    columns.start()

    def split(value, base):
        high = value.astype(BF16)
        rhs[base:base + 512, 0:128] = high
        rhs[base:base + 512, 128:256] = (value - high.astype(F32)).astype(BF16)

    split(density(core), 0)
    families.wait()
    fill_hot(family2, 4)

    counts = jnp.zeros((8, 128), F32)
    for ref in (family, family2):
        for g in range(4):
            row = ref[g:g + 1, :]
            high = one_hot(lax.broadcasted_iota(jnp.int32, (8, 128), 0) == (row >> 7))
            low = one_hot(lax.broadcasted_iota(jnp.int32, (128, 128), 0) == (row & 127))
            counts += lax.dot_general(high, low, (((1,), (1,)), ((), ())), preferred_element_type=F32)

    columns.wait()
    split(recv0[...], 512)

    def family_sums(half, block):
        at = pl.multiple_of(half * 512 + block * 128, 128)
        both = lax.dot_general(hot[pl.ds(at, 128), :], rhs[...], (((1,), (0,)), ((), ())), preferred_element_type=F32)
        return both[:, 0:128] + both[:, 128:256]

    def exchange(send, recv, half, p, ssem, rsem, device):
        return pltpu.make_async_remote_copy(
            send.at[p - 1], recv.at[p - 1], ssem.at[half, p - 1], rsem.at[half, p - 1],
            device_id=device, device_id_type=MESH,
        )

    first = {}
    for p in (2, 1, 3):
        sendx0[p - 1, 0:128, :] = family_sums(0, lax.rem(x + p, 4))
        sendx0[p - 1, 128:136, :] = counts
        first[0, p] = exchange(sendx0, recvx0, 0, p, ssem1, rsem1, along_x(p))
        first[0, p].start()
        sendx1[p - 1, 0:128, :] = family_sums(1, lax.rem(y + p, 4))
        first[1, p] = exchange(sendx1, recvx1, 1, p, ssem1, rsem1, along_y(p))
        first[1, p].start()
    recvx0[3, 0:128, :] = family_sums(0, x)
    recvx0[3, 128:136, :] = counts
    recvx1[3, 0:128, :] = family_sums(1, y)

    second = {}
    for half in (0, 1):
        recv, send, other, into, device = (
            (recvx0, sendy0, y, recvy0, along_y) if half == 0 else (recvx1, sendy1, x, recvy1, along_x)
        )
        for p in (1, 2, 3):
            first[half, p].wait()
        if half == 0:
            counts = recv[0, 128:136, :] + recv[1, 128:136, :] + recv[2, 128:136, :] + recv[3, 128:136, :]

        def block(b):
            at = pl.ds(pl.multiple_of(b * 32, 32), 32)
            return (recv[0, at, :] + recv[1, at, :]) + (recv[2, at, :] + recv[3, at, :])

        for p in (2, 1, 3):
            send[p - 1, 0:32, :] = block(lax.rem(other + p, 4))
            if half == 0:
                send[p - 1, 32:40, :] = counts
            second[half, p] = exchange(send, into, half, p, ssem2, rsem2, device(p))
            second[half, p].start()
        into[3, 0:32, :] = block(other)
        if half == 0:
            into[3, 32:40, :] = counts

    for half in (0, 1):
        recv = (recvy0, recvy1)[half]
        for p in (1, 2, 3):
            second[half, p].wait()
        value = (recv[0] + recv[1]) + (recv[2] + recv[3])
        for b in range(4):
            sendz[b, half * 8:half * 8 + 8, :] = value[b * 8:b * 8 + 8, :]
            if half == 0:
                sendz[b, 16:24, :] = value[32:40, :]

    third = []
    for p in list(range(1, 16)):
        device, q = along_z(p)
        block = lax.div(q, 8) * 2 + lax.rem(q, 2)
        copy = pltpu.make_async_remote_copy(
            sendz.at[block], recvz.at[spot], ssem3.at[p], rsem3.at[spot], device_id=device, device_id_type=MESH
        )
        copy.start()
        third.append(copy)
    recvz[spot] = sendz[zh * 2 + core]
    for p in range(1, 16):
        q = lax.rem(spot + p, 16)
        pltpu.make_async_remote_copy(
            sendz.at[0], recvz.at[q], ssem3.at[p], rsem3.at[q], device_id=sibling, device_id_type=MESH
        ).wait_recv()
    for copy in third:
        copy.wait_send()

    count_row = recvz[0, pl.ds(16 + lax.div(me, 8), 1), :] + recvz[8, pl.ds(16 + lax.div(me, 8), 1), :]
    lane = lax.broadcasted_iota(jnp.int32, (16, 128), 1)
    want = lax.broadcasted_iota(jnp.int32, (16, 128), 0) + lax.rem(me, 8) * 16
    count = jnp.sum(jnp.where(lane == want, jnp.broadcast_to(count_row, (16, 128)), 0.0), axis=1, keepdims=True)
    norm = 1.0 / jnp.sqrt(jnp.maximum(count, 1.0))
    for k in (0, 1):
        value = recvz[k, 0:16, :]
        for s in range(1, 8):
            value = value + recvz[2 * s + k, 0:16, :]
        out[:, k * 128:k * 128 + 128] = value * norm


def on_device(traces, primes, family, log_conductor):
    vmem = pl.BlockSpec(memory_space=pltpu.VMEM)
    dma = pltpu.SemaphoreType.DMA
    return pl.pallas_call(
        kernel,
        out_shape=jax.ShapeDtypeStruct((16, 256), F32),
        in_specs=[pl.BlockSpec(memory_space=pl.ANY), vmem, vmem, vmem],
        out_specs=vmem,
        scratch_shapes=[
            pltpu.VMEM((STEPS, ROWS, CHUNK), jnp.int32),
            pltpu.VMEM((48, 128), F32),
            pltpu.VMEM((48, 128), F32),
            pltpu.VMEM((48, 128), F32),
            pltpu.VMEM((256, CHUNK), BF16),
            pltpu.VMEM((ROWS, 256), F32),
            pltpu.VMEM((ROWS, 128), F32),
            pltpu.VMEM((FAMILIES, 1024), BF16),
            pltpu.VMEM((1024, 256), BF16),
            pltpu.VMEM((ROWS, 128), F32),
            pltpu.VMEM((ROWS, 128), F32),
            pltpu.VMEM((4, 128), jnp.int32),
            pltpu.VMEM((3, 136, 128), F32),
            pltpu.VMEM((3, 128, 128), F32),
            pltpu.VMEM((4, 136, 128), F32),
            pltpu.VMEM((4, 128, 128), F32),
            pltpu.VMEM((3, 40, 128), F32),
            pltpu.VMEM((3, 32, 128), F32),
            pltpu.VMEM((4, 40, 128), F32),
            pltpu.VMEM((4, 32, 128), F32),
            pltpu.VMEM((4, 24, 128), F32),
            pltpu.VMEM((16, 24, 128), F32),
            dma((STEPS,)),
            dma((2,)),
            dma((2,)),
            dma((2, 3)),
            dma((2, 3)),
            dma((2, 3)),
            dma((2, 3)),
            dma((16,)),
            dma((16,)),
        ],
        compiler_params=pltpu.CompilerParams(
            collective_id=0, has_side_effects=True, vmem_limit_bytes=56 << 20
        ),
        name="profile",
    )(traces, primes.reshape(48, 128), family.reshape(4, 128), log_conductor.reshape(4, 128))


def solution(mesh):
    return jax.shard_map(
        on_device,
        mesh=mesh,
        in_specs=(P("curves", "primes"), P("primes"), P("curves"), P("curves")),
        out_specs=P("curves", None),
        check_vma=False,
    )
```

```python
import jax
import jax.numpy as jnp
from jax import lax
from jax.experimental import pallas as pl
from jax.experimental.pallas import tpu as pltpu
from jax.sharding import PartitionSpec as P

MESH = pl.DeviceIdType.MESH
ROWS = 512
DEPTH = 6144
CHUNK = 1024
STEPS = DEPTH // CHUNK
GROUPS = CHUNK // 128
FAMILIES = 1024
BLOCK = 256
MEET = 2
F32 = jnp.float32
BF16 = jnp.bfloat16
PIECES = ((0, 0, 32), (1, 0, 32))


def times(a, b):
    return a[0] * b[0] - a[1] * b[1], a[0] * b[1] + a[1] * b[0]


def one_hot(cond):
    return jnp.where(cond, 1.0, 0.0).astype(BF16)


def kernel(
    traces, primes_in, family_in, conductor_in, out,
    tr, primes, family, conductor, inverse, base_cos, base_sin, weight, table, total, factor, hot, rhs, send0, recv0, family2,
    sums, plane_in, column, column_in, count, count_in,
    copy_sem, small_sem, ssem0, rsem0, ssem1, rsem1, ssem2, rsem2, csend, crecv,
):
    me = lax.axis_index("curves")
    zl = lax.axis_index("primes")
    core = lax.rem(me, 2)
    x = lax.rem(lax.div(me, 2), 4)
    zh = lax.rem(lax.div(me, 8), 2)
    y = lax.div(me, 16)

    def curve(y, zh, x, core):
        return ((y * 2 + zh) * 4 + x) * 2 + core

    def in_plane(dx, dy):
        return (curve(lax.rem(y + dy, 4), zh, lax.rem(x + dx, 4), core), zl)

    spot = (zh * 4 + zl) * 2 + core

    def in_column(z_hi, z_lo, k):
        return (curve(y, z_hi, x, k), z_lo)

    sibling = (curve(y, zh, x, 1 - core), zl)

    def remote(src, dst, ssem, rsem, device):
        return pltpu.make_async_remote_copy(src, dst, ssem, rsem, device_id=device, device_id_type=MESH)

    def fetch(i):
        return pltpu.make_async_copy(
            traces.at[:, pl.ds(pl.multiple_of(i * CHUNK, CHUNK), CHUNK)], tr.at[i], copy_sem.at[i]
        )

    def repeat(first, last, do):
        def body(i, carry):
            do(i)
            return carry

        lax.fori_loop(first, last, body, 0)

    small = [
        pltpu.make_async_copy(a, b, small_sem.at[j])
        for j, (a, b) in enumerate(((primes_in, primes), (family_in, family), (conductor_in, conductor)))
    ]
    for copy in small:
        copy.start()
    repeat(0, STEPS, lambda i: fetch(i).start())

    def plane_peer(e):
        return in_plane(lax.rem(e, 4), lax.div(e, 4))

    def column_peer(e):
        q = lax.rem(spot + e, 16)
        return in_column(lax.div(q, 8), lax.rem(lax.div(q, 2), 4), lax.rem(q, 2))

    barrier = pltpu.get_barrier_semaphore()

    def greet(e):
        pl.semaphore_signal(barrier, inc=1, device_id=plane_peer(e), device_id_type=MESH)
        pl.semaphore_signal(barrier, inc=1, device_id=column_peer(e), device_id_type=MESH)

    repeat(1, 16, greet)

    for copy in small:
        copy.wait()

    prime = primes[...].astype(F32)
    log_prime = jnp.log(prime)
    weight[...] = log_prime / prime
    base_cos[...] = jnp.cos(log_prime * 0.5)
    base_sin[...] = jnp.sin(log_prime * 0.5)
    total[...] = jnp.zeros_like(total)

    sub = lax.broadcasted_iota(jnp.int32, (8, 128), 0)
    bits = [(sub & 1) != 0, (sub & 2) != 0, (sub & 4) != 0]

    def pick(mask, a):
        return jnp.where(mask, a[0], 1.0), jnp.where(mask, a[1], 0.0)

    def tables(row, lanes):
        z = (jnp.broadcast_to(base_cos[pl.ds(row, 1), :], (8, 128)), jnp.broadcast_to(base_sin[pl.ds(row, 1), :], (8, 128)))
        z2 = times(z, z)
        z4 = times(z2, z2)
        powers = [times(times(z, pick(bits[0], z)), times(pick(bits[1], z2), pick(bits[2], z4)))]
        step = times(z4, z4)
        for _ in range(4):
            powers = powers + [times(a, step) for a in powers]
            step = times(step, step)
        for part in (0, 1):
            table[part * 128:part * 128 + 128, lanes] = jnp.concatenate([a[part] for a in powers], axis=0).astype(BF16)

    def table_step(j):
        for u in range(2):
            tables(j * 2 + u, pl.ds(pl.multiple_of(j * 256 + u * 128, 128), 128))

    repeat(0, DEPTH // 256, table_step)

    def fill_hot(ref, at):
        def fill(b):
            rows = lax.broadcasted_iota(jnp.int32, (128, 128), 0) + lax.rem(b, 4) * 256 + lax.div(b, 4) * 128
            there = pl.ds(pl.multiple_of(b * 128, 128), 128)
            for g in range(4):
                row = jnp.broadcast_to(ref[g:g + 1, :], (128, 128))
                hot[there, (at + g) * 128:(at + g) * 128 + 128] = one_hot(rows == row)

        repeat(0, 8, fill)

    fill_hot(family, 0)

    inverse[...] = -2.0 / conductor[...]
    count[...] = jnp.zeros_like(count)

    def per_group(g):
        spread = jnp.broadcast_to(inverse[pl.ds(g, 1), :], (128, 128))
        factor[pl.ds(pl.multiple_of(g * 128, 128), 128), :] = jnp.transpose(spread)
        row = family[pl.ds(g, 1), :]
        high = one_hot(lax.broadcasted_iota(jnp.int32, (8, 128), 0) == (row >> 7))
        low = one_hot(lax.broadcasted_iota(jnp.int32, (128, 128), 0) == (row & 127))
        count[0] += lax.dot_general(high, low, (((1,), (1,)), ((), ())), preferred_element_type=F32)

    repeat(0, 4, per_group)

    families = remote(family, family2, ssem0.at[0], rsem0.at[0], sibling)

    def counting(stage, j):
        if stage == 0:
            device = in_plane(j + 1, 0)
        elif stage == 1:
            device = in_plane(0, j + 1)
        else:
            side = (lax.rem(zh + (j + 1) // 2, 2), lax.rem(core + (j + 1) % 2, 2))
            device = in_column(side[0], zl, side[1])
        return remote(count.at[stage], count_in.at[stage, j], csend.at[stage, j], crecv.at[stage, j], device)

    def count_start(stage):
        for j in range(3):
            counting(stage, j).start()

    def count_sum(stage):
        for j in range(3):
            counting(stage, j).wait()
        count[stage + 1] = (count[stage] + count_in[stage, 0]) + (count_in[stage, 1] + count_in[stage, 2])

    def trace_step(i):
        fetch(i).wait()
        w = jnp.concatenate([weight[pl.ds(i * GROUPS + g, 1), :] for g in range(GROUPS)], axis=1)
        coefficient = (tr[i].astype(F32) * w).astype(BF16)
        part = table[:, pl.ds(pl.multiple_of(i * CHUNK, CHUNK), CHUNK)]
        total[...] += lax.dot_general(coefficient, part, (((1,), (1,)), ((), ())), preferred_element_type=F32)

        @pl.when(i == MEET)
        def _():
            pl.semaphore_wait(barrier, 30)
            families.start()
            count_start(0)

        @pl.when(i == STEPS - 2)
        def _():
            families.wait()
            fill_hot(family2, 4)

    repeat(0, STEPS, trace_step)

    def density(k):
        return total[:, pl.ds(pl.multiple_of(k * 128, 128), 128)] * factor[...]

    def split(value, at):
        high = value.astype(BF16)
        rhs[at:at + ROWS, 0:128] = high
        rhs[at:at + ROWS, 128:256] = (value - high.astype(F32)).astype(BF16)

    def add_families(at, columns, fresh):
        there = pl.ds(pl.multiple_of(at, 128), BLOCK)
        both = lax.dot_general(
            hot[there, columns], rhs[columns, :], (((1,), (0,)), ((), ())), preferred_element_type=F32
        )
        value = both[:, 0:128] + both[:, 128:256]
        sums[there, :] = value if fresh else sums[there, :] + value

    send0[...] = density(1 - core)
    columns = remote(send0, recv0, ssem0.at[1], rsem0.at[1], sibling)
    columns.start()
    split(density(core), 0)
    repeat(0, FAMILIES // BLOCK, lambda b: add_families(b * BLOCK, slice(0, 512), True))
    count_sum(0)
    count_start(1)
    columns.wait()
    split(recv0[...], 512)

    mine = y * 4 + x

    def plane_copy(n, e):
        z_hi, first, rows = PIECES[n]
        block = lax.rem(y + lax.div(e, 4), 4) * 4 + lax.rem(x + lax.rem(e, 4), 4)
        at = pl.ds(pl.multiple_of(z_hi * 512 + block * 32 + first, 16), rows)
        return remote(
            sums.at[at, :], plane_in.at[z_hi, e, pl.ds(first, rows), :], ssem1.at[n, e], rsem1.at[n, e], plane_peer(e)
        )

    for n, (z_hi, first, rows) in enumerate(PIECES):
        if first == 0:
            repeat(0, 512 // BLOCK, lambda b: add_families(z_hi * 512 + b * BLOCK, slice(512, 1024), False))
        repeat(1, 16, lambda e: plane_copy(n, e).start())

    def column_copy(n, t):
        z_hi, first, rows = PIECES[n]
        k = lax.rem(t, 2) if rows == 32 else first // 16
        z_lo = lax.div(t, 2) if rows == 32 else t
        there = (z_hi * 4 + z_lo) * 2 + k
        block = column.at[z_hi, pl.ds(pl.multiple_of(k * 16, 16), 16), :]
        copy = remote(block, column_in.at[spot], ssem2.at[there], rsem2.at[spot], in_column(z_hi, z_lo, k))
        return there, copy

    def column_start(n, t):
        there, copy = column_copy(n, t)

        @pl.when(spot != there)
        def _():
            copy.start()

    def column_sent(n, t):
        there, copy = column_copy(n, t)

        @pl.when(spot != there)
        def _():
            copy.wait_send()

    def tree(parts):
        while len(parts) > 1:
            parts = [a + b for a, b in zip(parts[::2], parts[1::2])]
        return parts[0]

    for n, (z_hi, first, rows) in enumerate(PIECES):
        repeat(1, 16, lambda e: plane_copy(n, e).wait_recv())
        at = pl.multiple_of(z_hi * 512 + mine * 32 + first, 16)
        column[z_hi, first:first + rows, :] = tree(
            [sums[pl.ds(at, rows), :]] + [plane_in[z_hi, e, first:first + rows, :] for e in range(1, 16)]
        )
        repeat(0, 8 if rows == 32 else 4, lambda t: column_start(n, t))

    count_sum(1)
    count_start(2)

    column_in[spot] = column[zh, pl.ds(pl.multiple_of(core * 16, 16), 16), :]
    count_sum(2)
    count_row = count[3, pl.ds(lax.div(me, 8), 1), :]
    lane = lax.broadcasted_iota(jnp.int32, (16, 128), 1)
    want = lax.broadcasted_iota(jnp.int32, (16, 128), 0) + lax.rem(me, 8) * 16
    number = jnp.sum(jnp.where(lane == want, jnp.broadcast_to(count_row, (16, 128)), 0.0), axis=1, keepdims=True)
    norm = 1.0 / jnp.sqrt(jnp.maximum(number, 1.0))

    def arrived(t):
        q = lax.rem(spot + t, 16)
        remote(column.at[0, pl.ds(0, 16), :], column_in.at[q], ssem2.at[q], rsem2.at[q], sibling).wait_recv()

    repeat(1, 16, arrived)
    for k in (0, 1):
        out[:, k * 128:k * 128 + 128] = tree([column_in[2 * s + k] for s in range(8)]) * norm

    for n, (z_hi, first, rows) in enumerate(PIECES):
        repeat(0, 8 if rows == 32 else 4, lambda t: column_sent(n, t))
        repeat(1, 16, lambda e: plane_copy(n, e).wait_send())


def on_device(traces, primes, family, log_conductor):
    dma = pltpu.SemaphoreType.DMA
    hbm = pl.BlockSpec(memory_space=pl.ANY)
    return pl.pallas_call(
        kernel,
        out_shape=pltpu.VMEM((16, 256), F32),
        in_specs=[hbm, hbm, hbm, hbm],
        out_specs=pl.BlockSpec(memory_space=pltpu.VMEM),
        scratch_shapes=[
            pltpu.VMEM((STEPS, ROWS, CHUNK), jnp.int32),
            pltpu.VMEM((48, 128), jnp.int32),
            pltpu.VMEM((4, 128), jnp.int32),
            pltpu.VMEM((4, 128), F32),
            pltpu.VMEM((4, 128), F32),
            pltpu.VMEM((48, 128), F32),
            pltpu.VMEM((48, 128), F32),
            pltpu.VMEM((48, 128), F32),
            pltpu.VMEM((256, DEPTH), BF16),
            pltpu.VMEM((ROWS, 256), F32),
            pltpu.VMEM((ROWS, 128), F32),
            pltpu.VMEM((FAMILIES, 1024), BF16),
            pltpu.VMEM((1024, 256), BF16),
            pltpu.VMEM((ROWS, 128), F32),
            pltpu.VMEM((ROWS, 128), F32),
            pltpu.VMEM((4, 128), jnp.int32),
            pltpu.VMEM((FAMILIES, 128), F32),
            pltpu.VMEM((2, 16, 32, 128), F32),
            pltpu.VMEM((2, 32, 128), F32),
            pltpu.VMEM((16, 16, 128), F32),
            pltpu.VMEM((4, 8, 128), F32),
            pltpu.VMEM((3, 3, 8, 128), F32),
            dma((STEPS,)),
            dma((3,)),
            dma((2,)),
            dma((2,)),
            dma((len(PIECES), 16)),
            dma((len(PIECES), 16)),
            dma((16,)),
            dma((16,)),
            dma((3, 3)),
            dma((3, 3)),
        ],
        compiler_params=pltpu.CompilerParams(
            collective_id=0, has_side_effects=True, vmem_limit_bytes=56 << 20
        ),
        name="profile",
    )(traces, primes.reshape(48, 128), family.reshape(4, 128), log_conductor.reshape(4, 128))


def solution(mesh):
    return jax.shard_map(
        on_device,
        mesh=mesh,
        in_specs=(P("curves", "primes"), P("primes"), P("curves"), P("curves")),
        out_specs=P("curves", None),
        check_vma=False,
    )
```

```python
import jax
import jax.numpy as jnp
from jax import lax
from jax.experimental import pallas as pl
from jax.experimental.pallas import tpu as pltpu
from jax.sharding import PartitionSpec as P

MESH = pl.DeviceIdType.MESH
ROWS = 512
DEPTH = 6144
CHUNK = 1024
STEPS = DEPTH // CHUNK
GROUPS = CHUNK // 128
FAMILIES = 1024
BLOCK = 256
MEET = 2
F32 = jnp.float32
BF16 = jnp.bfloat16
PIECES = (0, 1)
ROTATE = 0


def times(a, b):
    return a[0] * b[0] - a[1] * b[1], a[0] * b[1] + a[1] * b[0]


def one_hot(cond):
    return jnp.where(cond, 1.0, 0.0).astype(BF16)


def kernel(
    traces, primes_in, family_in, conductor_in, out,
    tr, primes, family, conductor, inverse, base_cos, base_sin, weight, table, total, factor, hot, rhs, send0, recv0, family2,
    sums, plane_in, column, column_in, count, count_in,
    copy_sem, small_sem, ssem0, rsem0, ssem1, rsem1, ssem2, rsem2, csend, crecv,
):
    me = lax.axis_index("curves")
    zl = lax.axis_index("primes")
    core = lax.rem(me, 2)
    x = lax.rem(lax.div(me, 2), 4)
    zh = lax.rem(lax.div(me, 8), 2)
    y = lax.div(me, 16)

    def curve(y, zh, x, core):
        return ((y * 2 + zh) * 4 + x) * 2 + core

    def in_plane(dx, dy):
        return (curve(lax.rem(y + dy, 4), zh, lax.rem(x + dx, 4), core), zl)

    spot = (zh * 4 + zl) * 2 + core

    def in_column(z_hi, z_lo, k):
        return (curve(y, z_hi, x, k), z_lo)

    sibling = (curve(y, zh, x, 1 - core), zl)

    def remote(src, dst, ssem, rsem, device):
        return pltpu.make_async_remote_copy(src, dst, ssem, rsem, device_id=device, device_id_type=MESH)

    def fetch(i):
        return pltpu.make_async_copy(
            traces.at[:, pl.ds(pl.multiple_of(i * CHUNK, CHUNK), CHUNK)], tr.at[i], copy_sem.at[i]
        )

    def repeat(first, last, do):
        def body(i, carry):
            do(i)
            return carry

        lax.fori_loop(first, last, body, 0)

    small = [
        pltpu.make_async_copy(a, b, small_sem.at[j])
        for j, (a, b) in enumerate(((primes_in, primes), (family_in, family), (conductor_in, conductor)))
    ]
    for copy in small:
        copy.start()
    repeat(0, STEPS, lambda i: fetch(i).start())

    def plane_peer(e):
        return in_plane(lax.rem(e, 4), lax.div(e, 4))

    def column_peer(e):
        q = lax.rem(spot + e, 16)
        return in_column(lax.div(q, 8), lax.rem(lax.div(q, 2), 4), lax.rem(q, 2))

    barrier = pltpu.get_barrier_semaphore()

    def greet(e):
        pl.semaphore_signal(barrier, inc=1, device_id=plane_peer(e), device_id_type=MESH)
        pl.semaphore_signal(barrier, inc=1, device_id=column_peer(e), device_id_type=MESH)

    repeat(1, 16, greet)

    for copy in small:
        copy.wait()

    prime = primes[...].astype(F32)
    log_prime = jnp.log(prime)
    weight[...] = log_prime / prime
    base_cos[...] = jnp.cos(log_prime * 0.5)
    base_sin[...] = jnp.sin(log_prime * 0.5)
    total[...] = jnp.zeros_like(total)

    sub = lax.broadcasted_iota(jnp.int32, (8, 128), 0)
    bits = [(sub & 1) != 0, (sub & 2) != 0, (sub & 4) != 0]

    def pick(mask, a):
        return jnp.where(mask, a[0], 1.0), jnp.where(mask, a[1], 0.0)

    def tables(row, lanes):
        z = (jnp.broadcast_to(base_cos[pl.ds(row, 1), :], (8, 128)), jnp.broadcast_to(base_sin[pl.ds(row, 1), :], (8, 128)))
        z2 = times(z, z)
        z4 = times(z2, z2)
        powers = [times(times(z, pick(bits[0], z)), times(pick(bits[1], z2), pick(bits[2], z4)))]
        step = times(z4, z4)
        for _ in range(4):
            powers = powers + [times(a, step) for a in powers]
            step = times(step, step)
        for part in (0, 1):
            table[part * 128:part * 128 + 128, lanes] = jnp.concatenate([a[part] for a in powers], axis=0).astype(BF16)

    def table_step(j):
        for u in range(2):
            tables(j * 2 + u, pl.ds(pl.multiple_of(j * 256 + u * 128, 128), 128))

    repeat(0, DEPTH // 256, table_step)

    def fill_hot(ref, at):
        def fill(b):
            rows = lax.broadcasted_iota(jnp.int32, (128, 128), 0) + lax.rem(b, 4) * 256 + lax.div(b, 4) * 128
            there = pl.ds(pl.multiple_of(b * 128, 128), 128)
            for g in range(4):
                row = jnp.broadcast_to(ref[g:g + 1, :], (128, 128))
                hot[there, (at + g) * 128:(at + g) * 128 + 128] = one_hot(rows == row)

        repeat(0, 8, fill)

    fill_hot(family, 0)

    inverse[...] = -2.0 / conductor[...]
    count[...] = jnp.zeros_like(count)

    def per_group(g):
        spread = jnp.broadcast_to(inverse[pl.ds(g, 1), :], (128, 128))
        factor[pl.ds(pl.multiple_of(g * 128, 128), 128), :] = jnp.transpose(spread)
        row = family[pl.ds(g, 1), :]
        high = one_hot(lax.broadcasted_iota(jnp.int32, (8, 128), 0) == (row >> 7))
        low = one_hot(lax.broadcasted_iota(jnp.int32, (128, 128), 0) == (row & 127))
        count[0] += lax.dot_general(high, low, (((1,), (1,)), ((), ())), preferred_element_type=F32)

    repeat(0, 4, per_group)

    families = remote(family, family2, ssem0.at[0], rsem0.at[0], sibling)

    def counting(stage, j):
        if stage == 0:
            device = in_plane(j + 1, 0)
        elif stage == 1:
            device = in_plane(0, j + 1)
        else:
            side = (lax.rem(zh + (j + 1) // 2, 2), lax.rem(core + (j + 1) % 2, 2))
            device = in_column(side[0], zl, side[1])
        return remote(count.at[stage], count_in.at[stage, j], csend.at[stage, j], crecv.at[stage, j], device)

    def count_start(stage):
        for j in range(3):
            counting(stage, j).start()

    def count_sum(stage):
        for j in range(3):
            counting(stage, j).wait()
        count[stage + 1] = (count[stage] + count_in[stage, 0]) + (count_in[stage, 1] + count_in[stage, 2])

    def trace_step(i):
        fetch(i).wait()
        w = jnp.concatenate([weight[pl.ds(i * GROUPS + g, 1), :] for g in range(GROUPS)], axis=1)
        coefficient = (tr[i].astype(F32) * w).astype(BF16)
        part = table[:, pl.ds(pl.multiple_of(i * CHUNK, CHUNK), CHUNK)]
        total[...] += lax.dot_general(coefficient, part, (((1,), (1,)), ((), ())), preferred_element_type=F32)

        @pl.when(i == MEET)
        def _():
            pl.semaphore_wait(barrier, 30)
            families.start()
            count_start(0)

        @pl.when(i == STEPS - 2)
        def _():
            families.wait()
            fill_hot(family2, 4)

    repeat(0, STEPS, trace_step)

    def density(k):
        return total[:, pl.ds(pl.multiple_of(k * 128, 128), 128)] * factor[...]

    def split(value, at):
        high = value.astype(BF16)
        rhs[at:at + ROWS, 0:128] = high
        rhs[at:at + ROWS, 128:256] = (value - high.astype(F32)).astype(BF16)

    def add_families(at, columns, fresh):
        there = pl.ds(pl.multiple_of(at, 128), BLOCK)
        both = lax.dot_general(
            hot[there, columns], rhs[columns, :], (((1,), (0,)), ((), ())), preferred_element_type=F32
        )
        value = both[:, 0:128] + both[:, 128:256]
        sums[there, :] = value if fresh else sums[there, :] + value

    send0[...] = density(1 - core)
    columns = remote(send0, recv0, ssem0.at[1], rsem0.at[1], sibling)
    columns.start()
    split(density(core), 0)
    repeat(0, FAMILIES // BLOCK, lambda b: add_families(b * BLOCK, slice(0, 512), True))
    count_sum(0)
    count_start(1)
    columns.wait()
    split(recv0[...], 512)

    mine = y * 4 + x

    def plane_copy(n, i):
        z_hi = PIECES[n]
        b = lax.rem(i + ROTATE * mine, 16)
        at = pl.ds(pl.multiple_of(z_hi * 512 + b * 32, 32), 32)
        copy = remote(
            sums.at[at, :], plane_in.at[z_hi, mine], ssem1.at[n, b], rsem1.at[n, mine],
            (curve(lax.div(b, 4), zh, lax.rem(b, 4), core), zl),
        )
        return b, copy

    def plane_start(n, i):
        b, copy = plane_copy(n, i)

        @pl.when(b != mine)
        def _():
            copy.start()

    def plane_arrived(n, b):
        here = plane_in.at[PIECES[n], b]

        @pl.when(b != mine)
        def _():
            remote(here, here, ssem1.at[n, b], rsem1.at[n, b], sibling).wait_recv()

    def plane_sent(n, i):
        b, copy = plane_copy(n, i)

        @pl.when(b != mine)
        def _():
            copy.wait_send()

    def plane_scatter(n):
        z_hi = PIECES[n]
        repeat(0, 16, lambda i: plane_start(n, i))
        plane_in[z_hi, mine] = sums[pl.ds(pl.multiple_of(z_hi * 512 + mine * 32, 32), 32), :]

    def finish_families(n):
        repeat(0, 512 // BLOCK, lambda b: add_families(PIECES[n] * 512 + b * BLOCK, slice(512, 1024), False))

    def column_copy(n, t):
        z_hi = PIECES[n]
        k = 1 - lax.rem(t, 2)
        there = z_hi * 8 + lax.div(t, 2) * 2 + k
        block = column.at[z_hi, pl.ds(pl.multiple_of(k * 16, 16), 16), :]
        copy = remote(
            block, column_in.at[spot], ssem2.at[there], rsem2.at[spot], in_column(z_hi, lax.div(t, 2), k)
        )
        return there, copy

    def column_start(n, t):
        there, copy = column_copy(n, t)

        @pl.when(spot != there)
        def _():
            copy.start()

    def column_sent(n, t):
        there, copy = column_copy(n, t)

        @pl.when(spot != there)
        def _():
            copy.wait_send()

    def tree(parts):
        while len(parts) > 1:
            parts = [a + b for a, b in zip(parts[::2], parts[1::2])]
        return parts[0]

    def plane_gather(n):
        z_hi = PIECES[n]
        repeat(0, 16, lambda b: plane_arrived(n, b))
        column[z_hi] = tree([plane_in[z_hi, b] for b in range(16)])
        repeat(0, 8, lambda t: column_start(n, t))

    finish_families(0)
    plane_scatter(0)
    finish_families(1)
    count_sum(1)
    count_start(2)
    plane_gather(0)
    plane_scatter(1)
    plane_gather(1)

    column_in[spot] = column[zh, pl.ds(pl.multiple_of(core * 16, 16), 16), :]
    count_sum(2)
    count_row = count[3, pl.ds(lax.div(me, 8), 1), :]
    lane = lax.broadcasted_iota(jnp.int32, (16, 128), 1)
    want = lax.broadcasted_iota(jnp.int32, (16, 128), 0) + lax.rem(me, 8) * 16
    number = jnp.sum(jnp.where(lane == want, jnp.broadcast_to(count_row, (16, 128)), 0.0), axis=1, keepdims=True)
    norm = 1.0 / jnp.sqrt(jnp.maximum(number, 1.0))

    def arrived(t):
        q = lax.rem(spot + t, 16)
        remote(column.at[0, pl.ds(0, 16), :], column_in.at[q], ssem2.at[q], rsem2.at[q], sibling).wait_recv()

    repeat(1, 16, arrived)
    for k in (0, 1):
        out[:, k * 128:k * 128 + 128] = tree([column_in[2 * s + k] for s in range(8)]) * norm

    for n in range(2):
        repeat(0, 8, lambda t: column_sent(n, t))
        repeat(0, 16, lambda i: plane_sent(n, i))


def on_device(traces, primes, family, log_conductor):
    dma = pltpu.SemaphoreType.DMA
    hbm = pl.BlockSpec(memory_space=pl.ANY)
    return pl.pallas_call(
        kernel,
        out_shape=pltpu.VMEM((16, 256), F32),
        in_specs=[hbm, hbm, hbm, hbm],
        out_specs=pl.BlockSpec(memory_space=pltpu.VMEM),
        scratch_shapes=[
            pltpu.VMEM((STEPS, ROWS, CHUNK), jnp.int32),
            pltpu.VMEM((48, 128), jnp.int32),
            pltpu.VMEM((4, 128), jnp.int32),
            pltpu.VMEM((4, 128), F32),
            pltpu.VMEM((4, 128), F32),
            pltpu.VMEM((48, 128), F32),
            pltpu.VMEM((48, 128), F32),
            pltpu.VMEM((48, 128), F32),
            pltpu.VMEM((256, DEPTH), BF16),
            pltpu.VMEM((ROWS, 256), F32),
            pltpu.VMEM((ROWS, 128), F32),
            pltpu.VMEM((FAMILIES, 1024), BF16),
            pltpu.VMEM((1024, 256), BF16),
            pltpu.VMEM((ROWS, 128), F32),
            pltpu.VMEM((ROWS, 128), F32),
            pltpu.VMEM((4, 128), jnp.int32),
            pltpu.VMEM((FAMILIES, 128), F32),
            pltpu.VMEM((2, 16, 32, 128), F32),
            pltpu.VMEM((2, 32, 128), F32),
            pltpu.VMEM((16, 16, 128), F32),
            pltpu.VMEM((4, 8, 128), F32),
            pltpu.VMEM((3, 3, 8, 128), F32),
            dma((STEPS,)),
            dma((3,)),
            dma((2,)),
            dma((2,)),
            dma((len(PIECES), 16)),
            dma((len(PIECES), 16)),
            dma((16,)),
            dma((16,)),
            dma((3, 3)),
            dma((3, 3)),
        ],
        compiler_params=pltpu.CompilerParams(
            collective_id=0, has_side_effects=True, vmem_limit_bytes=56 << 20
        ),
        name="profile",
    )(traces, primes.reshape(48, 128), family.reshape(4, 128), log_conductor.reshape(4, 128))


def solution(mesh):
    return jax.shard_map(
        on_device,
        mesh=mesh,
        in_specs=(P("curves", "primes"), P("primes"), P("curves"), P("curves")),
        out_specs=P("curves", None),
        check_vma=False,
    )
```

```python
import jax
import jax.numpy as jnp
from jax import lax
from jax.experimental import pallas as pl
from jax.experimental.pallas import tpu as pltpu
from jax.sharding import PartitionSpec as P

MESH = pl.DeviceIdType.MESH
ROWS = 512
DEPTH = 6144
CHUNK = 2048
STEPS = DEPTH // CHUNK
GROUPS = CHUNK // 128
FAMILIES = 1024
BLOCK = 256
MEET = 1
F32 = jnp.float32
BF16 = jnp.bfloat16
PIECES = (0, 1)
ROTATE = 0


def times(a, b):
    return a[0] * b[0] - a[1] * b[1], a[0] * b[1] + a[1] * b[0]


def one_hot(cond):
    return jnp.where(cond, 1.0, 0.0).astype(BF16)


def kernel(
    traces, primes_in, family_in, conductor_in, out,
    tr, primes, family, conductor, inverse, base_cos, base_sin, weight, table, total, factor, hot, rhs, send0, recv0, family2,
    sums, plane_in, column, column_in, count, count_in,
    copy_sem, small_sem, ssem0, rsem0, ssem1, rsem1, ssem2, rsem2, csend, crecv,
):
    me = lax.axis_index("curves")
    zl = lax.axis_index("primes")
    core = lax.rem(me, 2)
    x = lax.rem(lax.div(me, 2), 4)
    zh = lax.rem(lax.div(me, 8), 2)
    y = lax.div(me, 16)

    def curve(y, zh, x, core):
        return ((y * 2 + zh) * 4 + x) * 2 + core

    def in_plane(dx, dy):
        return (curve(lax.rem(y + dy, 4), zh, lax.rem(x + dx, 4), core), zl)

    spot = (zh * 4 + zl) * 2 + core

    def in_column(z_hi, z_lo, k):
        return (curve(y, z_hi, x, k), z_lo)

    sibling = (curve(y, zh, x, 1 - core), zl)

    def remote(src, dst, ssem, rsem, device):
        return pltpu.make_async_remote_copy(src, dst, ssem, rsem, device_id=device, device_id_type=MESH)

    def fetch(i):
        return pltpu.make_async_copy(
            traces.at[:, pl.ds(pl.multiple_of(i * CHUNK, CHUNK), CHUNK)], tr.at[i], copy_sem.at[i]
        )

    def repeat(first, last, do):
        def body(i, carry):
            do(i)
            return carry

        lax.fori_loop(first, last, body, 0)

    small = [
        pltpu.make_async_copy(a, b, small_sem.at[j])
        for j, (a, b) in enumerate(((primes_in, primes), (family_in, family), (conductor_in, conductor)))
    ]
    for copy in small:
        copy.start()
    repeat(0, STEPS, lambda i: fetch(i).start())

    def plane_peer(e):
        return in_plane(lax.rem(e, 4), lax.div(e, 4))

    def column_peer(e):
        q = lax.rem(spot + e, 16)
        return in_column(lax.div(q, 8), lax.rem(lax.div(q, 2), 4), lax.rem(q, 2))

    barrier = pltpu.get_barrier_semaphore()

    def greet(e):
        pl.semaphore_signal(barrier, inc=1, device_id=plane_peer(e), device_id_type=MESH)
        pl.semaphore_signal(barrier, inc=1, device_id=column_peer(e), device_id_type=MESH)

    repeat(1, 16, greet)

    for copy in small:
        copy.wait()

    prime = primes[...].astype(F32)
    log_prime = jnp.log(prime)
    weight[...] = log_prime / prime
    base_cos[...] = jnp.cos(log_prime * 0.5)
    base_sin[...] = jnp.sin(log_prime * 0.5)
    total[...] = jnp.zeros_like(total)

    sub = lax.broadcasted_iota(jnp.int32, (8, 128), 0)
    bits = [(sub & 1) != 0, (sub & 2) != 0, (sub & 4) != 0]

    def pick(mask, a):
        return jnp.where(mask, a[0], 1.0), jnp.where(mask, a[1], 0.0)

    def tables(row, lanes):
        z = (jnp.broadcast_to(base_cos[pl.ds(row, 1), :], (8, 128)), jnp.broadcast_to(base_sin[pl.ds(row, 1), :], (8, 128)))
        z2 = times(z, z)
        z4 = times(z2, z2)
        powers = [times(times(z, pick(bits[0], z)), times(pick(bits[1], z2), pick(bits[2], z4)))]
        step = times(z4, z4)
        for _ in range(4):
            powers = powers + [times(a, step) for a in powers]
            step = times(step, step)
        for part in (0, 1):
            table[part * 128:part * 128 + 128, lanes] = jnp.concatenate([a[part] for a in powers], axis=0).astype(BF16)

    def table_step(j):
        for u in range(2):
            tables(j * 2 + u, pl.ds(pl.multiple_of(j * 256 + u * 128, 128), 128))

    repeat(0, DEPTH // 256, table_step)

    def fill_hot(ref, at):
        def fill(b):
            rows = lax.broadcasted_iota(jnp.int32, (128, 128), 0) + lax.rem(b, 4) * 256 + lax.div(b, 4) * 128
            there = pl.ds(pl.multiple_of(b * 128, 128), 128)
            for g in range(4):
                row = jnp.broadcast_to(ref[g:g + 1, :], (128, 128))
                hot[there, (at + g) * 128:(at + g) * 128 + 128] = one_hot(rows == row)

        repeat(0, 8, fill)

    fill_hot(family, 0)

    inverse[...] = -2.0 / conductor[...]
    count[...] = jnp.zeros_like(count)

    def per_group(g):
        spread = jnp.broadcast_to(inverse[pl.ds(g, 1), :], (128, 128))
        factor[pl.ds(pl.multiple_of(g * 128, 128), 128), :] = jnp.transpose(spread)
        row = family[pl.ds(g, 1), :]
        high = one_hot(lax.broadcasted_iota(jnp.int32, (8, 128), 0) == (row >> 7))
        low = one_hot(lax.broadcasted_iota(jnp.int32, (128, 128), 0) == (row & 127))
        count[0] += lax.dot_general(high, low, (((1,), (1,)), ((), ())), preferred_element_type=F32)

    repeat(0, 4, per_group)

    families = remote(family, family2, ssem0.at[0], rsem0.at[0], sibling)

    def counting(stage, j):
        if stage == 0:
            device = in_plane(j + 1, 0)
        elif stage == 1:
            device = in_plane(0, j + 1)
        else:
            side = (lax.rem(zh + (j + 1) // 2, 2), lax.rem(core + (j + 1) % 2, 2))
            device = in_column(side[0], zl, side[1])
        return remote(count.at[stage], count_in.at[stage, j], csend.at[stage, j], crecv.at[stage, j], device)

    def count_start(stage):
        for j in range(3):
            counting(stage, j).start()

    def count_sum(stage):
        for j in range(3):
            counting(stage, j).wait()
        count[stage + 1] = (count[stage] + count_in[stage, 0]) + (count_in[stage, 1] + count_in[stage, 2])

    def trace_step(i):
        fetch(i).wait()
        w = jnp.concatenate([weight[pl.ds(i * GROUPS + g, 1), :] for g in range(GROUPS)], axis=1)
        coefficient = (tr[i].astype(F32) * w).astype(BF16)
        part = table[:, pl.ds(pl.multiple_of(i * CHUNK, CHUNK), CHUNK)]
        total[...] += lax.dot_general(coefficient, part, (((1,), (1,)), ((), ())), preferred_element_type=F32)

        @pl.when(i == MEET)
        def _():
            pl.semaphore_wait(barrier, 30)
            families.start()
            count_start(0)

    repeat(0, STEPS, trace_step)

    def density(k):
        return total[:, pl.ds(pl.multiple_of(k * 128, 128), 128)] * factor[...]

    def split(value, at):
        high = value.astype(BF16)
        rhs[at:at + ROWS, 0:128] = high
        rhs[at:at + ROWS, 128:256] = (value - high.astype(F32)).astype(BF16)

    def add_families(at, columns, fresh):
        there = pl.ds(pl.multiple_of(at, 128), BLOCK)
        both = lax.dot_general(
            hot[there, columns], rhs[columns, :], (((1,), (0,)), ((), ())), preferred_element_type=F32
        )
        value = both[:, 0:128] + both[:, 128:256]
        sums[there, :] = value if fresh else sums[there, :] + value

    send0[...] = density(1 - core)
    columns = remote(send0, recv0, ssem0.at[1], rsem0.at[1], sibling)
    columns.start()
    split(density(core), 0)
    repeat(0, FAMILIES // BLOCK, lambda b: add_families(b * BLOCK, slice(0, 512), True))
    families.wait()
    fill_hot(family2, 4)
    count_sum(0)
    count_start(1)
    columns.wait()
    split(recv0[...], 512)

    mine = y * 4 + x

    def plane_copy(n, i):
        z_hi = PIECES[n]
        b = lax.rem(i + ROTATE * mine, 16)
        at = pl.ds(pl.multiple_of(z_hi * 512 + b * 32, 32), 32)
        copy = remote(
            sums.at[at, :], plane_in.at[z_hi, mine], ssem1.at[n, b], rsem1.at[n, mine],
            (curve(lax.div(b, 4), zh, lax.rem(b, 4), core), zl),
        )
        return b, copy

    def plane_start(n, i):
        b, copy = plane_copy(n, i)

        @pl.when(b != mine)
        def _():
            copy.start()

    def plane_arrived(n, b):
        here = plane_in.at[PIECES[n], b]

        @pl.when(b != mine)
        def _():
            remote(here, here, ssem1.at[n, b], rsem1.at[n, b], sibling).wait_recv()

    def plane_sent(n, i):
        b, copy = plane_copy(n, i)

        @pl.when(b != mine)
        def _():
            copy.wait_send()

    def plane_scatter(n):
        z_hi = PIECES[n]
        repeat(0, 16, lambda i: plane_start(n, i))
        plane_in[z_hi, mine] = sums[pl.ds(pl.multiple_of(z_hi * 512 + mine * 32, 32), 32), :]

    def finish_families(n):
        repeat(0, 512 // BLOCK, lambda b: add_families(PIECES[n] * 512 + b * BLOCK, slice(512, 1024), False))

    def column_copy(n, t):
        z_hi = PIECES[n]
        k = 1 - lax.rem(t, 2)
        there = z_hi * 8 + lax.div(t, 2) * 2 + k
        block = column.at[z_hi, pl.ds(pl.multiple_of(k * 16, 16), 16), :]
        copy = remote(
            block, column_in.at[spot], ssem2.at[there], rsem2.at[spot], in_column(z_hi, lax.div(t, 2), k)
        )
        return there, copy

    def column_start(n, t):
        there, copy = column_copy(n, t)

        @pl.when(spot != there)
        def _():
            copy.start()

    def column_sent(n, t):
        there, copy = column_copy(n, t)

        @pl.when(spot != there)
        def _():
            copy.wait_send()

    def tree(parts):
        while len(parts) > 1:
            parts = [a + b for a, b in zip(parts[::2], parts[1::2])]
        return parts[0]

    def plane_gather(n):
        z_hi = PIECES[n]
        repeat(0, 16, lambda b: plane_arrived(n, b))
        column[z_hi] = tree([plane_in[z_hi, b] for b in range(16)])
        repeat(0, 8, lambda t: column_start(n, t))

    finish_families(0)
    plane_scatter(0)
    finish_families(1)
    count_sum(1)
    count_start(2)
    plane_gather(0)
    plane_scatter(1)
    plane_gather(1)

    column_in[spot] = column[zh, pl.ds(pl.multiple_of(core * 16, 16), 16), :]
    count_sum(2)
    count_row = count[3, pl.ds(lax.div(me, 8), 1), :]
    lane = lax.broadcasted_iota(jnp.int32, (16, 128), 1)
    want = lax.broadcasted_iota(jnp.int32, (16, 128), 0) + lax.rem(me, 8) * 16
    number = jnp.sum(jnp.where(lane == want, jnp.broadcast_to(count_row, (16, 128)), 0.0), axis=1, keepdims=True)
    norm = 1.0 / jnp.sqrt(jnp.maximum(number, 1.0))

    def arrived(t):
        q = lax.rem(spot + t, 16)
        remote(column.at[0, pl.ds(0, 16), :], column_in.at[q], ssem2.at[q], rsem2.at[q], sibling).wait_recv()

    repeat(1, 16, arrived)
    for k in (0, 1):
        out[:, k * 128:k * 128 + 128] = tree([column_in[2 * s + k] for s in range(8)]) * norm

    for n in range(2):
        repeat(0, 8, lambda t: column_sent(n, t))
        repeat(0, 16, lambda i: plane_sent(n, i))


def on_device(traces, primes, family, log_conductor):
    dma = pltpu.SemaphoreType.DMA
    hbm = pl.BlockSpec(memory_space=pl.ANY)
    return pl.pallas_call(
        kernel,
        out_shape=pltpu.VMEM((16, 256), F32),
        in_specs=[hbm, hbm, hbm, hbm],
        out_specs=pl.BlockSpec(memory_space=pltpu.VMEM),
        scratch_shapes=[
            pltpu.VMEM((STEPS, ROWS, CHUNK), jnp.int32),
            pltpu.VMEM((48, 128), jnp.int32),
            pltpu.VMEM((4, 128), jnp.int32),
            pltpu.VMEM((4, 128), F32),
            pltpu.VMEM((4, 128), F32),
            pltpu.VMEM((48, 128), F32),
            pltpu.VMEM((48, 128), F32),
            pltpu.VMEM((48, 128), F32),
            pltpu.VMEM((256, DEPTH), BF16),
            pltpu.VMEM((ROWS, 256), F32),
            pltpu.VMEM((ROWS, 128), F32),
            pltpu.VMEM((FAMILIES, 1024), BF16),
            pltpu.VMEM((1024, 256), BF16),
            pltpu.VMEM((ROWS, 128), F32),
            pltpu.VMEM((ROWS, 128), F32),
            pltpu.VMEM((4, 128), jnp.int32),
            pltpu.VMEM((FAMILIES, 128), F32),
            pltpu.VMEM((2, 16, 32, 128), F32),
            pltpu.VMEM((2, 32, 128), F32),
            pltpu.VMEM((16, 16, 128), F32),
            pltpu.VMEM((4, 8, 128), F32),
            pltpu.VMEM((3, 3, 8, 128), F32),
            dma((STEPS,)),
            dma((3,)),
            dma((2,)),
            dma((2,)),
            dma((len(PIECES), 16)),
            dma((len(PIECES), 16)),
            dma((16,)),
            dma((16,)),
            dma((3, 3)),
            dma((3, 3)),
        ],
        compiler_params=pltpu.CompilerParams(
            collective_id=0, has_side_effects=True, vmem_limit_bytes=56 << 20
        ),
        name="profile",
    )(traces, primes.reshape(48, 128), family.reshape(4, 128), log_conductor.reshape(4, 128))


def solution(mesh):
    return jax.shard_map(
        on_device,
        mesh=mesh,
        in_specs=(P("curves", "primes"), P("primes"), P("curves"), P("curves")),
        out_specs=P("curves", None),
        check_vma=False,
    )
```

```python
import jax
import jax.numpy as jnp
from jax import lax
from jax.experimental import pallas as pl
from jax.experimental.pallas import tpu as pltpu
from jax.sharding import PartitionSpec as P

MESH = pl.DeviceIdType.MESH
ROWS = 512
DEPTH = 6144
CHUNK = 2048
STEPS = DEPTH // CHUNK
GROUPS = CHUNK // 128
FAMILIES = 1024
BLOCK = 256
MEET = 1
F32 = jnp.float32
BF16 = jnp.bfloat16
PIECES = (0, 1)
ROTATE = 0


def times(a, b):
    return a[0] * b[0] - a[1] * b[1], a[0] * b[1] + a[1] * b[0]


def one_hot(cond):
    return jnp.where(cond, 1.0, 0.0).astype(BF16)


def kernel(
    traces, primes_in, family_in, conductor_in, out,
    tr, primes, family, conductor, base_cos, base_sin, weight, table, total, factor, hot, rhs, send0, recv0, family2,
    sums, plane_in, column, column_in, count, count_in,
    copy_sem, small_sem, ssem0, rsem0, ssem1, rsem1, ssem2, rsem2, csend, crecv,
):
    me = lax.axis_index("curves")
    zl = lax.axis_index("primes")
    core = lax.rem(me, 2)
    x = lax.rem(lax.div(me, 2), 4)
    zh = lax.rem(lax.div(me, 8), 2)
    y = lax.div(me, 16)

    def curve(y, zh, x, core):
        return ((y * 2 + zh) * 4 + x) * 2 + core

    def in_plane(dx, dy):
        return (curve(lax.rem(y + dy, 4), zh, lax.rem(x + dx, 4), core), zl)

    spot = (zh * 4 + zl) * 2 + core

    def in_column(z_hi, z_lo, k):
        return (curve(y, z_hi, x, k), z_lo)

    sibling = (curve(y, zh, x, 1 - core), zl)

    def remote(src, dst, ssem, rsem, device):
        return pltpu.make_async_remote_copy(src, dst, ssem, rsem, device_id=device, device_id_type=MESH)

    def fetch(i):
        return pltpu.make_async_copy(
            traces.at[:, pl.ds(pl.multiple_of(i * CHUNK, CHUNK), CHUNK)], tr.at[i], copy_sem.at[i]
        )

    def repeat(first, last, do):
        def body(i, carry):
            do(i)
            return carry

        lax.fori_loop(first, last, body, 0)

    small = [
        pltpu.make_async_copy(a, b, small_sem.at[j])
        for j, (a, b) in enumerate(((primes_in, primes), (family_in, family), (conductor_in, conductor)))
    ]
    for copy in small:
        copy.start()
    repeat(0, STEPS, lambda i: fetch(i).start())

    def plane_peer(e):
        return in_plane(lax.rem(e, 4), lax.div(e, 4))

    def column_peer(e):
        q = lax.rem(spot + e, 16)
        return in_column(lax.div(q, 8), lax.rem(lax.div(q, 2), 4), lax.rem(q, 2))

    barrier = pltpu.get_barrier_semaphore()

    def greet(e):
        pl.semaphore_signal(barrier, inc=1, device_id=plane_peer(e), device_id_type=MESH)
        pl.semaphore_signal(barrier, inc=1, device_id=column_peer(e), device_id_type=MESH)

    repeat(1, 16, greet)

    for copy in small:
        copy.wait()

    prime = primes[...].astype(F32)
    log_prime = jnp.log(prime)
    weight[...] = log_prime / prime
    base_cos[...] = jnp.cos(log_prime * 0.5)
    base_sin[...] = jnp.sin(log_prime * 0.5)
    total[...] = jnp.zeros_like(total)

    sub = lax.broadcasted_iota(jnp.int32, (8, 128), 0)
    bits = [(sub & 1) != 0, (sub & 2) != 0, (sub & 4) != 0]

    def pick(mask, a):
        return jnp.where(mask, a[0], 1.0), jnp.where(mask, a[1], 0.0)

    def tables(row, lanes):
        z = (jnp.broadcast_to(base_cos[pl.ds(row, 1), :], (8, 128)), jnp.broadcast_to(base_sin[pl.ds(row, 1), :], (8, 128)))
        z2 = times(z, z)
        z4 = times(z2, z2)
        powers = [times(times(z, pick(bits[0], z)), times(pick(bits[1], z2), pick(bits[2], z4)))]
        step = times(z4, z4)
        for _ in range(4):
            powers = powers + [times(a, step) for a in powers]
            step = times(step, step)
        for part in (0, 1):
            table[part * 128:part * 128 + 128, lanes] = jnp.concatenate([a[part] for a in powers], axis=0).astype(BF16)

    def table_step(j):
        for u in range(2):
            tables(j * 2 + u, pl.ds(pl.multiple_of(j * 256 + u * 128, 128), 128))

    repeat(0, DEPTH // 256, table_step)

    def fill_hot(ref, at):
        def fill(b):
            rows = lax.broadcasted_iota(jnp.int32, (128, 128), 0) + lax.rem(b, 4) * 256 + lax.div(b, 4) * 128
            there = pl.ds(pl.multiple_of(b * 128, 128), 128)
            for g in range(4):
                row = jnp.broadcast_to(ref[g:g + 1, :], (128, 128))
                hot[there, (at + g) * 128:(at + g) * 128 + 128] = one_hot(rows == row)

        repeat(0, 8, fill)

    fill_hot(family, 0)

    inverse = -2.0 / conductor[...]
    for g in range(4):
        factor[g * 128:g * 128 + 128, :] = jnp.transpose(jnp.broadcast_to(inverse[g:g + 1, :], (128, 128)))

    row = jnp.concatenate([family[g:g + 1, :] for g in range(4)], axis=1)
    high = one_hot(lax.broadcasted_iota(jnp.int32, (8, ROWS), 0) == (row >> 7))
    low = one_hot(lax.broadcasted_iota(jnp.int32, (128, ROWS), 0) == (row & 127))
    count[0] = lax.dot_general(high, low, (((1,), (1,)), ((), ())), preferred_element_type=F32)

    families = remote(family, family2, ssem0.at[0], rsem0.at[0], sibling)

    def counting(stage, j):
        if stage == 0:
            device = in_plane(j + 1, 0)
        elif stage == 1:
            device = in_plane(0, j + 1)
        else:
            side = (lax.rem(zh + (j + 1) // 2, 2), lax.rem(core + (j + 1) % 2, 2))
            device = in_column(side[0], zl, side[1])
        return remote(count.at[stage], count_in.at[stage, j], csend.at[stage, j], crecv.at[stage, j], device)

    def count_start(stage):
        for j in range(3):
            counting(stage, j).start()

    def count_sum(stage):
        for j in range(3):
            counting(stage, j).wait()
        count[stage + 1] = (count[stage] + count_in[stage, 0]) + (count_in[stage, 1] + count_in[stage, 2])

    def trace_step(i):
        fetch(i).wait()
        w = jnp.concatenate([weight[pl.ds(i * GROUPS + g, 1), :] for g in range(GROUPS)], axis=1)
        coefficient = (tr[i].astype(F32) * w).astype(BF16)
        part = table[:, pl.ds(pl.multiple_of(i * CHUNK, CHUNK), CHUNK)]
        total[...] += lax.dot_general(coefficient, part, (((1,), (1,)), ((), ())), preferred_element_type=F32)

        @pl.when(i == MEET)
        def _():
            pl.semaphore_wait(barrier, 30)
            families.start()
            count_start(0)

    repeat(0, STEPS, trace_step)

    def density(k):
        return total[:, pl.ds(pl.multiple_of(k * 128, 128), 128)] * factor[...]

    def split(value, at):
        high = value.astype(BF16)
        rhs[at:at + ROWS, 0:128] = high
        rhs[at:at + ROWS, 128:256] = (value - high.astype(F32)).astype(BF16)

    def add_families(at, columns, fresh):
        there = pl.ds(pl.multiple_of(at, 128), BLOCK)
        both = lax.dot_general(
            hot[there, columns], rhs[columns, :], (((1,), (0,)), ((), ())), preferred_element_type=F32
        )
        value = both[:, 0:128] + both[:, 128:256]
        sums[there, :] = value if fresh else sums[there, :] + value

    send0[...] = density(1 - core)
    columns = remote(send0, recv0, ssem0.at[1], rsem0.at[1], sibling)
    columns.start()
    split(density(core), 0)
    repeat(0, FAMILIES // BLOCK, lambda b: add_families(b * BLOCK, slice(0, 512), True))
    families.wait()
    fill_hot(family2, 4)
    count_sum(0)
    count_start(1)
    columns.wait()
    split(recv0[...], 512)

    mine = y * 4 + x

    def plane_copy(n, i):
        z_hi = PIECES[n]
        b = lax.rem(i + ROTATE * mine, 16)
        at = pl.ds(pl.multiple_of(z_hi * 512 + b * 32, 32), 32)
        copy = remote(
            sums.at[at, :], plane_in.at[z_hi, mine], ssem1.at[n, b], rsem1.at[n, mine],
            (curve(lax.div(b, 4), zh, lax.rem(b, 4), core), zl),
        )
        return b, copy

    def plane_start(n, i):
        b, copy = plane_copy(n, i)

        @pl.when(b != mine)
        def _():
            copy.start()

    def plane_arrived(n, b):
        here = plane_in.at[PIECES[n], b]

        @pl.when(b != mine)
        def _():
            remote(here, here, ssem1.at[n, b], rsem1.at[n, b], sibling).wait_recv()

    def plane_sent(n, i):
        b, copy = plane_copy(n, i)

        @pl.when(b != mine)
        def _():
            copy.wait_send()

    def plane_scatter(n):
        z_hi = PIECES[n]
        repeat(0, 16, lambda i: plane_start(n, i))
        plane_in[z_hi, mine] = sums[pl.ds(pl.multiple_of(z_hi * 512 + mine * 32, 32), 32), :]

    def finish_families(n):
        repeat(0, 512 // BLOCK, lambda b: add_families(PIECES[n] * 512 + b * BLOCK, slice(512, 1024), False))

    def column_copy(n, t):
        z_hi = PIECES[n]
        k = 1 - lax.rem(t, 2)
        there = z_hi * 8 + lax.div(t, 2) * 2 + k
        block = column.at[z_hi, pl.ds(pl.multiple_of(k * 16, 16), 16), :]
        copy = remote(
            block, column_in.at[spot], ssem2.at[there], rsem2.at[spot], in_column(z_hi, lax.div(t, 2), k)
        )
        return there, copy

    def column_start(n, t):
        there, copy = column_copy(n, t)

        @pl.when(spot != there)
        def _():
            copy.start()

    def column_sent(n, t):
        there, copy = column_copy(n, t)

        @pl.when(spot != there)
        def _():
            copy.wait_send()

    def tree(parts):
        while len(parts) > 1:
            parts = [a + b for a, b in zip(parts[::2], parts[1::2])]
        return parts[0]

    def plane_gather(n):
        z_hi = PIECES[n]
        repeat(0, 16, lambda b: plane_arrived(n, b))
        column[z_hi] = tree([plane_in[z_hi, b] for b in range(16)])
        repeat(0, 8, lambda t: column_start(n, t))

    finish_families(0)
    plane_scatter(0)
    finish_families(1)
    count_sum(1)
    count_start(2)
    plane_gather(0)
    plane_scatter(1)
    plane_gather(1)

    column_in[spot] = column[zh, pl.ds(pl.multiple_of(core * 16, 16), 16), :]
    count_sum(2)
    count_row = count[3, pl.ds(lax.div(me, 8), 1), :]
    lane = lax.broadcasted_iota(jnp.int32, (16, 128), 1)
    want = lax.broadcasted_iota(jnp.int32, (16, 128), 0) + lax.rem(me, 8) * 16
    number = jnp.sum(jnp.where(lane == want, jnp.broadcast_to(count_row, (16, 128)), 0.0), axis=1, keepdims=True)
    norm = 1.0 / jnp.sqrt(jnp.maximum(number, 1.0))

    def arrived(t):
        q = lax.rem(spot + t, 16)
        remote(column.at[0, pl.ds(0, 16), :], column_in.at[q], ssem2.at[q], rsem2.at[q], sibling).wait_recv()

    for n in range(len(PIECES)):
        repeat(0, 16, lambda i: plane_sent(n, i))
        repeat(0, 8, lambda t: column_sent(n, t))
    repeat(1, 16, arrived)
    for k in (0, 1):
        out[:, k * 128:k * 128 + 128] = tree([column_in[2 * s + k] for s in range(8)]) * norm


def on_device(traces, primes, family, log_conductor):
    dma = pltpu.SemaphoreType.DMA
    hbm = pl.BlockSpec(memory_space=pl.ANY)
    return pl.pallas_call(
        kernel,
        out_shape=pltpu.VMEM((16, 256), F32),
        in_specs=[hbm, hbm, hbm, hbm],
        out_specs=pl.BlockSpec(memory_space=pltpu.VMEM),
        scratch_shapes=[
            pltpu.VMEM((STEPS, ROWS, CHUNK), jnp.int32),
            pltpu.VMEM((48, 128), jnp.int32),
            pltpu.VMEM((4, 128), jnp.int32),
            pltpu.VMEM((4, 128), F32),
            pltpu.VMEM((48, 128), F32),
            pltpu.VMEM((48, 128), F32),
            pltpu.VMEM((48, 128), F32),
            pltpu.VMEM((256, DEPTH), BF16),
            pltpu.VMEM((ROWS, 256), F32),
            pltpu.VMEM((ROWS, 128), F32),
            pltpu.VMEM((FAMILIES, 1024), BF16),
            pltpu.VMEM((1024, 256), BF16),
            pltpu.VMEM((ROWS, 128), F32),
            pltpu.VMEM((ROWS, 128), F32),
            pltpu.VMEM((4, 128), jnp.int32),
            pltpu.VMEM((FAMILIES, 128), F32),
            pltpu.VMEM((2, 16, 32, 128), F32),
            pltpu.VMEM((2, 32, 128), F32),
            pltpu.VMEM((16, 16, 128), F32),
            pltpu.VMEM((4, 8, 128), F32),
            pltpu.VMEM((3, 3, 8, 128), F32),
            dma((STEPS,)),
            dma((3,)),
            dma((2,)),
            dma((2,)),
            dma((len(PIECES), 16)),
            dma((len(PIECES), 16)),
            dma((16,)),
            dma((16,)),
            dma((3, 3)),
            dma((3, 3)),
        ],
        compiler_params=pltpu.CompilerParams(
            collective_id=0, has_side_effects=True, vmem_limit_bytes=56 << 20
        ),
        name="profile",
    )(traces, primes.reshape(48, 128), family.reshape(4, 128), log_conductor.reshape(4, 128))


def solution(mesh):
    return jax.shard_map(
        on_device,
        mesh=mesh,
        in_specs=(P("curves", "primes"), P("primes"), P("curves"), P("curves")),
        out_specs=P("curves", None),
        check_vma=False,
    )
```

```python
import jax
import jax.numpy as jnp
from jax import lax
from jax.experimental import pallas as pl
from jax.experimental.pallas import tpu as pltpu
from jax.sharding import PartitionSpec as P

MESH = pl.DeviceIdType.MESH
ROWS = 512
DEPTH = 6144
CHUNK = 2048
STEPS = DEPTH // CHUNK
GROUPS = CHUNK // 128
FAMILIES = 1024
BLOCK = 512
MEET = 1
F32 = jnp.float32
BF16 = jnp.bfloat16
PIECES = (0, 1)
ROTATE = 0


def times(a, b):
    return a[0] * b[0] - a[1] * b[1], a[0] * b[1] + a[1] * b[0]


def one_hot(cond):
    return jnp.where(cond, 1.0, 0.0).astype(BF16)


def kernel(
    traces, primes_in, family_in, conductor_in, out,
    tr, primes, family, conductor, base_cos, base_sin, weight, table, total, factor, hot, rhs, send0, recv0, family2,
    sums, plane_in, column, column_in, count, count_in,
    copy_sem, small_sem, ssem0, rsem0, ssem1, rsem1, ssem2, rsem2, csend, crecv,
):
    me = lax.axis_index("curves")
    zl = lax.axis_index("primes")
    core = lax.rem(me, 2)
    x = lax.rem(lax.div(me, 2), 4)
    zh = lax.rem(lax.div(me, 8), 2)
    y = lax.div(me, 16)

    def curve(y, zh, x, core):
        return ((y * 2 + zh) * 4 + x) * 2 + core

    def in_plane(dx, dy):
        return (curve(lax.rem(y + dy, 4), zh, lax.rem(x + dx, 4), core), zl)

    spot = (zh * 4 + zl) * 2 + core

    def in_column(z_hi, z_lo, k):
        return (curve(y, z_hi, x, k), z_lo)

    sibling = (curve(y, zh, x, 1 - core), zl)

    def remote(src, dst, ssem, rsem, device):
        return pltpu.make_async_remote_copy(src, dst, ssem, rsem, device_id=device, device_id_type=MESH)

    def fetch(i):
        return pltpu.make_async_copy(
            traces.at[:, pl.ds(pl.multiple_of(i * CHUNK, CHUNK), CHUNK)], tr.at[i], copy_sem.at[i]
        )

    def repeat(first, last, do):
        def body(i, carry):
            do(i)
            return carry

        lax.fori_loop(first, last, body, 0)

    small = [
        pltpu.make_async_copy(a, b, small_sem.at[j])
        for j, (a, b) in enumerate(((primes_in, primes), (family_in, family), (conductor_in, conductor)))
    ]
    for copy in small:
        copy.start()
    repeat(0, STEPS, lambda i: fetch(i).start())

    def plane_peer(e):
        return in_plane(lax.rem(e, 4), lax.div(e, 4))

    def column_peer(e):
        q = lax.rem(spot + e, 16)
        return in_column(lax.div(q, 8), lax.rem(lax.div(q, 2), 4), lax.rem(q, 2))

    barrier = pltpu.get_barrier_semaphore()

    def greet(e):
        pl.semaphore_signal(barrier, inc=1, device_id=plane_peer(e), device_id_type=MESH)
        pl.semaphore_signal(barrier, inc=1, device_id=column_peer(e), device_id_type=MESH)

    repeat(1, 16, greet)

    for copy in small:
        copy.wait()

    prime = primes[...].astype(F32)
    log_prime = jnp.log(prime)
    weight[...] = log_prime / prime
    base_cos[...] = jnp.cos(log_prime * 0.5)
    base_sin[...] = jnp.sin(log_prime * 0.5)
    total[...] = jnp.zeros_like(total)

    sub = lax.broadcasted_iota(jnp.int32, (8, 128), 0)
    bits = [(sub & 1) != 0, (sub & 2) != 0, (sub & 4) != 0]

    def pick(mask, a):
        return jnp.where(mask, a[0], 1.0), jnp.where(mask, a[1], 0.0)

    def tables(row, lanes):
        z = (jnp.broadcast_to(base_cos[pl.ds(row, 1), :], (8, 128)), jnp.broadcast_to(base_sin[pl.ds(row, 1), :], (8, 128)))
        z2 = times(z, z)
        z4 = times(z2, z2)
        powers = [times(times(z, pick(bits[0], z)), times(pick(bits[1], z2), pick(bits[2], z4)))]
        step = times(z4, z4)
        for _ in range(4):
            powers = powers + [times(a, step) for a in powers]
            step = times(step, step)
        for part in (0, 1):
            table[part * 128:part * 128 + 128, lanes] = jnp.concatenate([a[part] for a in powers], axis=0).astype(BF16)

    def table_step(j):
        for u in range(2):
            tables(j * 2 + u, pl.ds(pl.multiple_of(j * 256 + u * 128, 128), 128))

    repeat(0, DEPTH // 256, table_step)

    def fill_hot(ref, at):
        def fill(b):
            rows = lax.broadcasted_iota(jnp.int32, (128, 128), 0) + lax.rem(b, 4) * 256 + lax.div(b, 4) * 128
            there = pl.ds(pl.multiple_of(b * 128, 128), 128)
            for g in range(4):
                row = jnp.broadcast_to(ref[g:g + 1, :], (128, 128))
                hot[there, (at + g) * 128:(at + g) * 128 + 128] = one_hot(rows == row)

        repeat(0, 8, fill)

    fill_hot(family, 0)

    inverse = -2.0 / conductor[...]
    for g in range(4):
        factor[g * 128:g * 128 + 128, :] = jnp.transpose(jnp.broadcast_to(inverse[g:g + 1, :], (128, 128)))

    row = jnp.concatenate([family[g:g + 1, :] for g in range(4)], axis=1)
    high = one_hot(lax.broadcasted_iota(jnp.int32, (8, ROWS), 0) == (row >> 7))
    low = one_hot(lax.broadcasted_iota(jnp.int32, (128, ROWS), 0) == (row & 127))
    count[0] = lax.dot_general(high, low, (((1,), (1,)), ((), ())), preferred_element_type=F32)

    families = remote(family, family2, ssem0.at[0], rsem0.at[0], sibling)

    def counting(stage, j):
        if stage == 0:
            device = in_plane(j + 1, 0)
        elif stage == 1:
            device = in_plane(0, j + 1)
        else:
            side = (lax.rem(zh + (j + 1) // 2, 2), lax.rem(core + (j + 1) % 2, 2))
            device = in_column(side[0], zl, side[1])
        return remote(count.at[stage], count_in.at[stage, j], csend.at[stage, j], crecv.at[stage, j], device)

    def count_start(stage):
        for j in range(3):
            counting(stage, j).start()

    def count_sum(stage):
        for j in range(3):
            counting(stage, j).wait()
        count[stage + 1] = (count[stage] + count_in[stage, 0]) + (count_in[stage, 1] + count_in[stage, 2])

    def trace_step(i):
        fetch(i).wait()
        w = jnp.concatenate([weight[pl.ds(i * GROUPS + g, 1), :] for g in range(GROUPS)], axis=1)
        coefficient = (tr[i].astype(F32) * w).astype(BF16)
        part = table[:, pl.ds(pl.multiple_of(i * CHUNK, CHUNK), CHUNK)]
        total[...] += lax.dot_general(coefficient, part, (((1,), (1,)), ((), ())), preferred_element_type=F32)

        @pl.when(i == MEET)
        def _():
            pl.semaphore_wait(barrier, 30)
            families.start()
            count_start(0)

    repeat(0, STEPS, trace_step)

    def density(k):
        return total[:, pl.ds(pl.multiple_of(k * 128, 128), 128)] * factor[...]

    def split(value, at):
        high = value.astype(BF16)
        rhs[at:at + ROWS, 0:128] = high
        rhs[at:at + ROWS, 128:256] = (value - high.astype(F32)).astype(BF16)

    def add_families(at, columns, fresh):
        there = pl.ds(pl.multiple_of(at, 128), BLOCK)
        both = lax.dot_general(
            hot[there, columns], rhs[columns, :], (((1,), (0,)), ((), ())), preferred_element_type=F32
        )
        value = both[:, 0:128] + both[:, 128:256]
        sums[there, :] = value if fresh else sums[there, :] + value

    send0[...] = density(1 - core)
    columns = remote(send0, recv0, ssem0.at[1], rsem0.at[1], sibling)
    columns.start()
    split(density(core), 0)
    repeat(0, FAMILIES // BLOCK, lambda b: add_families(b * BLOCK, slice(0, 512), True))
    families.wait()
    fill_hot(family2, 4)
    count_sum(0)
    count_start(1)
    columns.wait()
    split(recv0[...], 512)

    mine = y * 4 + x

    def plane_copy(n, i):
        z_hi = PIECES[n]
        b = lax.rem(i + ROTATE * mine, 16)
        at = pl.ds(pl.multiple_of(z_hi * 512 + b * 32, 32), 32)
        copy = remote(
            sums.at[at, :], plane_in.at[z_hi, mine], ssem1.at[n, b], rsem1.at[n, mine],
            (curve(lax.div(b, 4), zh, lax.rem(b, 4), core), zl),
        )
        return b, copy

    def plane_start(n, i):
        b, copy = plane_copy(n, i)

        @pl.when(b != mine)
        def _():
            copy.start()

    def plane_arrived(n, b):
        here = plane_in.at[PIECES[n], b]

        @pl.when(b != mine)
        def _():
            remote(here, here, ssem1.at[n, b], rsem1.at[n, b], sibling).wait_recv()

    def plane_sent(n, i):
        b, copy = plane_copy(n, i)

        @pl.when(b != mine)
        def _():
            copy.wait_send()

    def plane_scatter(n):
        z_hi = PIECES[n]
        repeat(0, 16, lambda i: plane_start(n, i))
        plane_in[z_hi, mine] = sums[pl.ds(pl.multiple_of(z_hi * 512 + mine * 32, 32), 32), :]

    def finish_families(n):
        repeat(0, 512 // BLOCK, lambda b: add_families(PIECES[n] * 512 + b * BLOCK, slice(512, 1024), False))

    def column_copy(n, t):
        z_hi = PIECES[n]
        k = 1 - lax.rem(t, 2)
        there = z_hi * 8 + lax.div(t, 2) * 2 + k
        block = column.at[z_hi, pl.ds(pl.multiple_of(k * 16, 16), 16), :]
        copy = remote(
            block, column_in.at[spot], ssem2.at[there], rsem2.at[spot], in_column(z_hi, lax.div(t, 2), k)
        )
        return there, copy

    def column_start(n, t):
        there, copy = column_copy(n, t)

        @pl.when(spot != there)
        def _():
            copy.start()

    def column_sent(n, t):
        there, copy = column_copy(n, t)

        @pl.when(spot != there)
        def _():
            copy.wait_send()

    def tree(parts):
        while len(parts) > 1:
            parts = [a + b for a, b in zip(parts[::2], parts[1::2])]
        return parts[0]

    def plane_gather(n):
        z_hi = PIECES[n]
        repeat(0, 16, lambda b: plane_arrived(n, b))
        column[z_hi] = tree([plane_in[z_hi, b] for b in range(16)])
        repeat(0, 8, lambda t: column_start(n, t))

    finish_families(0)
    plane_scatter(0)
    finish_families(1)
    count_sum(1)
    count_start(2)
    plane_gather(0)
    plane_scatter(1)
    plane_gather(1)

    column_in[spot] = column[zh, pl.ds(pl.multiple_of(core * 16, 16), 16), :]
    count_sum(2)
    count_row = count[3, pl.ds(lax.div(me, 8), 1), :]
    lane = lax.broadcasted_iota(jnp.int32, (16, 128), 1)
    want = lax.broadcasted_iota(jnp.int32, (16, 128), 0) + lax.rem(me, 8) * 16
    number = jnp.sum(jnp.where(lane == want, jnp.broadcast_to(count_row, (16, 128)), 0.0), axis=1, keepdims=True)
    norm = 1.0 / jnp.sqrt(jnp.maximum(number, 1.0))

    def arrived(t):
        q = lax.rem(spot + t, 16)
        remote(column.at[0, pl.ds(0, 16), :], column_in.at[q], ssem2.at[q], rsem2.at[q], sibling).wait_recv()

    for n in range(len(PIECES)):
        repeat(0, 16, lambda i: plane_sent(n, i))
        repeat(0, 8, lambda t: column_sent(n, t))
    repeat(1, 16, arrived)
    for k in (0, 1):
        out[:, k * 128:k * 128 + 128] = tree([column_in[2 * s + k] for s in range(8)]) * norm


def on_device(traces, primes, family, log_conductor):
    dma = pltpu.SemaphoreType.DMA
    hbm = pl.BlockSpec(memory_space=pl.ANY)
    return pl.pallas_call(
        kernel,
        out_shape=pltpu.VMEM((16, 256), F32),
        in_specs=[hbm, hbm, hbm, hbm],
        out_specs=pl.BlockSpec(memory_space=pltpu.VMEM),
        scratch_shapes=[
            pltpu.VMEM((STEPS, ROWS, CHUNK), jnp.int32),
            pltpu.VMEM((48, 128), jnp.int32),
            pltpu.VMEM((4, 128), jnp.int32),
            pltpu.VMEM((4, 128), F32),
            pltpu.VMEM((48, 128), F32),
            pltpu.VMEM((48, 128), F32),
            pltpu.VMEM((48, 128), F32),
            pltpu.VMEM((256, DEPTH), BF16),
            pltpu.VMEM((ROWS, 256), F32),
            pltpu.VMEM((ROWS, 128), F32),
            pltpu.VMEM((FAMILIES, 1024), BF16),
            pltpu.VMEM((1024, 256), BF16),
            pltpu.VMEM((ROWS, 128), F32),
            pltpu.VMEM((ROWS, 128), F32),
            pltpu.VMEM((4, 128), jnp.int32),
            pltpu.VMEM((FAMILIES, 128), F32),
            pltpu.VMEM((2, 16, 32, 128), F32),
            pltpu.VMEM((2, 32, 128), F32),
            pltpu.VMEM((16, 16, 128), F32),
            pltpu.VMEM((4, 8, 128), F32),
            pltpu.VMEM((3, 3, 8, 128), F32),
            dma((STEPS,)),
            dma((3,)),
            dma((2,)),
            dma((2,)),
            dma((len(PIECES), 16)),
            dma((len(PIECES), 16)),
            dma((16,)),
            dma((16,)),
            dma((3, 3)),
            dma((3, 3)),
        ],
        compiler_params=pltpu.CompilerParams(
            collective_id=0, has_side_effects=True, vmem_limit_bytes=56 << 20
        ),
        name="profile",
    )(traces, primes.reshape(48, 128), family.reshape(4, 128), log_conductor.reshape(4, 128))


def solution(mesh):
    return jax.shard_map(
        on_device,
        mesh=mesh,
        in_specs=(P("curves", "primes"), P("primes"), P("curves"), P("curves")),
        out_specs=P("curves", None),
        check_vma=False,
    )
```
